512 devices in a mesh: wide: 64 (over z_hi, y, x, core), narrow: 8 (over z_lo).
Axes of the slice: x: 4, y: 4, z: 16 (z_hi: 2, z_lo: 8; z = z_hi * 8 + z_lo), core: 2. Of those that a mesh axis runs over, the one named last changes fastest.
Arguments:
- rhs: float32 [2, 50, 131072], P(None, None, ('wide', 'narrow')), may hold values from -6 to 6
- block_inv: float32 [50, 50, 131072], P(None, None, ('wide', 'narrow')), may hold values from -0.875 to 0.875
- line_order: int32 [512, 256], P(('wide', 'narrow')), may hold values from 0 to 255, each once within a row
- line_coef: float32 [2, 131072], P(None, ('wide', 'narrow')), may hold values from 0.2 to 1
- line_faces: float32 [2, 50, 50], replicated, may hold values from -0.875 to 0.875
- intersection: int32 [512, 4, 128], P(('wide', 'narrow')), may hold values from 0 to 255
- intersection_coef: float32 [512, 4, 128], P(('wide', 'narrow')), may hold values from 0.2 to 1
- ghost_face: float32 [50, 50], replicated, may hold values from -0.875 to 0.875
- modes: float32 [131072, 384], P(('wide', 'narrow')), may hold values from -0.3125 to 0.3125
- coarse_inv: float32 [384, 384], replicated, may hold values from -0.015625 to 0.015625
Outputs:
- precond: float32 [2, 50, 131072], P(None, None, ('wide', 'narrow'))
The draws below stay inside these ranges and needn't reach their ends.
Inputs may be any that keep to these rules, and one draw needn't show every extreme that they name: Each row of line_order lists each of the 256 local elements once. `intersection`: entries are local element numbers of their own subdomain; an element may appear several times.
All inputs are finite; a program needn't handle non-finite values.
Results may differ from the reference program's by a relative error of at most 0.0003.
Values sent between devices are 32-bit elements; how exact they have to be, the bound alone decides.
No kernel may reach another device: no remote copies, remote signals or barrier semaphores. Data moves between devices by JAX's collectives and lax.ppermute only.
A program may use at most 64 MiB of HBM per device.

```python
import math
import jax
import jax.numpy as jnp
import numpy as np
from jax import lax

NDOF = 50
LINE = 32
E_DEV = 256
OV = 128
KC = 384
NSUB = 512
ELEMS = 131072
N_NARROW = 8


def set_ends(entries, own_key, least, largest):
    index_at = [jax.random.randint(jax.random.fold_in(own_key, axis), (), 0, length) for axis, length in enumerate(entries.shape)]
    main_axis = entries.shape.index(max(entries.shape))
    neighbour = index_at[:main_axis] + [(index_at[main_axis] + 1) % entries.shape[main_axis]] + index_at[main_axis + 1:]
    return entries.at[tuple(index_at)].set(least).at[tuple(neighbour)].set(largest)


def block_scale(rng, dims, pieces, low, top_value):
    def one(position, shards_of):
        steps = jax.random.uniform(jax.random.fold_in(jax.random.fold_in(rng, 6), position), (shards_of,), jnp.float32, low / len(pieces), top_value / len(pieces))
        return jnp.repeat(jnp.exp(steps), dims[position] // shards_of).reshape((-1,) + (1,) * (len(dims) - position - 1))

    level = one(*pieces[0])
    for cut in pieces[1:]:
        level = level * one(*cut)
    return level


def bell_draw(rng, shape, deviation, limit, cuts=(), kind=jnp.bfloat16):
    values = jax.random.normal(rng, shape, jnp.float32) * deviation
    if len(cuts) > 0:
        values = block_scale(rng, shape, cuts, -0.22, 0.18) * values
    return jnp.clip(values, min=-limit, max=limit).astype(kind)


def setup_inputs(seed: int = 0) -> dict:
    splits = jax.random.split(jax.random.key(seed), 11)
    rhs = bell_draw(splits[0], (2, NDOF, ELEMS), 1.0, 6.0, ((2, 512),), jnp.float32)
    block_inv = bell_draw(splits[1], (NDOF, NDOF, ELEMS), NDOF ** -0.5, 0.875, ((2, 512),), jnp.float32)
    line_order = jax.vmap(lambda own: jax.random.permutation(own, E_DEV))(jax.random.split(splits[2], NSUB)).reshape((NSUB, E_DEV)).astype(jnp.int32)
    line_coef = jnp.clip(jnp.exp(math.log(1.0) - 1.609438 * jax.random.uniform(splits[3], (2, ELEMS), jnp.float32) ** block_scale(splits[3], (2, ELEMS), ((1, 512),), -0.2, 0.2)), 0.2, 1.0)
    line_faces = bell_draw(splits[4], (2, NDOF, NDOF), NDOF ** -0.5, 0.875, (), jnp.float32)
    intersection = set_ends(jax.random.randint(splits[5], (NSUB, 4, OV), 0, E_DEV), jax.random.fold_in(splits[5], 1), 0, E_DEV - 1).astype(jnp.int32)
    intersection_coef = jnp.clip(jnp.exp(math.log(1.0) - 1.609438 * jax.random.uniform(splits[6], (NSUB, 4, OV), jnp.float32) ** block_scale(splits[6], (NSUB, 4, OV), ((0, 512),), -0.2, 0.2)), 0.2, 1.0)
    ghost_face = bell_draw(splits[7], (NDOF, NDOF), NDOF ** -0.5, 0.875, (), jnp.float32)
    modes = bell_draw(splits[8], (ELEMS, KC), KC ** -0.5, 0.3125, ((0, 512),), jnp.float32)
    coarse_inv = bell_draw(splits[9], (KC, KC), (E_DEV * NSUB) ** -0.5, 0.015625, (), jnp.float32)
    return {"rhs": rhs, "block_inv": block_inv, "line_order": line_order, "line_coef": line_coef, "line_faces": line_faces, "intersection": intersection, "intersection_coef": intersection_coef, "ghost_face": ghost_face, "modes": modes, "coarse_inv": coarse_inv}


def colour_rows(vector, layers):
    return jnp.stack([jnp.take(vector, layers[colour], axis=1) for colour in range(4)])


def boosted_rhs(vector, layers, weights, received, ghost_face):
    pushed = jnp.einsum("ij,cjk->cik", ghost_face, received, precision=lax.Precision.HIGHEST) * weights[:, None, :]
    columns = jnp.transpose(pushed, (1, 0, 2)).reshape(vector.shape[0], -1)
    return vector.at[:, layers.reshape(-1)].add(columns)


def line_solve(vector, order, blocks, coefs, line_faces):
    ordered = jnp.take(vector, order, axis=1)
    first = jnp.einsum("ijp,jp->ip", blocks, ordered, precision=lax.Precision.HIGHEST)
    spot = jnp.arange(ordered.shape[1]) % LINE
    before = jnp.where(spot[None, :] > 0, jnp.roll(first, 1, axis=1), 0.0)
    after = jnp.where(spot[None, :] < LINE - 1, jnp.roll(first, -1, axis=1), 0.0)
    coupled = ordered + coefs[0] * jnp.dot(line_faces[0], before, precision=lax.Precision.HIGHEST)
    coupled = coupled + coefs[1] * jnp.dot(line_faces[1], after, precision=lax.Precision.HIGHEST)
    second = jnp.einsum("ijp,jp->ip", blocks, coupled, precision=lax.Precision.HIGHEST)
    return jnp.zeros_like(vector).at[:, order].set(second)


def reference(rhs, block_inv, line_order, line_coef, line_faces, intersection, intersection_coef, ghost_face, modes, coarse_inv):
    wide_index = np.arange(NSUB) // N_NARROW
    narrow_index = np.arange(NSUB) % N_NARROW
    partners = [((wide_index ^ (1 << colour)) * N_NARROW + narrow_index).astype(np.int32) for colour in range(4)]
    stacked = jnp.transpose(rhs.reshape(2, NDOF, NSUB, E_DEV), (0, 2, 1, 3))
    sent = jax.vmap(lambda per_app: jax.vmap(colour_rows)(per_app, intersection))(stacked)
    received = jnp.stack([sent[:, partners[colour], colour] for colour in range(4)], axis=2)

    def per_sub(index):
        start = (index * E_DEV).astype(jnp.int32)
        blocks = lax.dynamic_slice_in_dim(block_inv, start, E_DEV, 2)
        coefs = lax.dynamic_slice_in_dim(line_coef, start, E_DEV, 1)
        results = []
        for app in range(2):
            vector = stacked[app, index]
            lifted = boosted_rhs(vector, intersection[index], intersection_coef[index], received[app, index], ghost_face)
            results.append(line_solve(lifted, line_order[index], blocks, coefs, line_faces))
        return jnp.stack(results)

    local = lax.map(per_sub, jnp.arange(NSUB, dtype=jnp.int32))
    local = jnp.transpose(local, (1, 2, 0, 3)).reshape(2, NDOF, NSUB * E_DEV)
    coarse_res = jnp.einsum("aje,ek->ajk", rhs, modes, precision=lax.Precision.HIGHEST)
    coarse_sol = jnp.einsum("ajk,kl->ajl", coarse_res, coarse_inv, precision=lax.Precision.HIGHEST)
    return local + jnp.einsum("ajl,el->aje", coarse_sol, modes, precision=lax.Precision.HIGHEST)
```

```python
import jax
import jax.numpy as jnp
import numpy as np
from jax import lax
from jax.sharding import PartitionSpec as P

LINE = 32
ALL = ("wide", "narrow")
PLANE = 32
RING = 16
ROWS = 4
HI = lax.Precision.HIGHEST


def groups():
    place = np.arange(PLANE * RING).reshape(2, PLANE, 8)
    plane = place.transpose(0, 2, 1).reshape(-1, PLANE).tolist()
    ring = place.transpose(1, 0, 2).reshape(-1, RING).tolist()
    return plane, ring


def swap(blocks, groups_of):
    return lax.all_to_all(blocks, ALL, 0, 0, axis_index_groups=groups_of)


def flip(blocks, colour):
    half = 1 << colour
    shape = blocks.shape
    return blocks.reshape((-1, 2, half) + shape[1:])[:, ::-1].reshape(shape)


def shards(
    rhs,
    block_inv,
    line_order,
    line_coef,
    line_faces,
    intersection,
    intersection_coef,
    ghost_face,
    modes,
    coarse_inv,
):
    plane, ring = groups()
    order = line_order[0]
    layers = intersection[0].reshape(-1)
    weights = intersection_coef[0].reshape(-1)
    apps, ndof, count = rhs.shape
    kc = modes.shape[1]
    rows = apps * ndof
    ids = jnp.arange(count, dtype=jnp.int32)
    both = jnp.transpose(rhs, (1, 0, 2)).reshape(rows, count)
    pick = (ids[:, None] == layers[None, :]).astype(jnp.float32)
    front = jnp.dot(both, jnp.concatenate([modes, pick], axis=1), precision=HI)
    out0 = jnp.pad(front, ((0, PLANE * ROWS - rows), (0, 0))).reshape(PLANE, ROWS, -1)
    in0 = swap(out0, plane)
    part = jnp.sum(in0[:, :, :kc], axis=0)
    in1 = swap(jnp.broadcast_to(part, (RING, ROWS, kc)), ring)
    coarse = jnp.sum(in1, axis=0)
    span = intersection.shape[2]
    pieces = [flip(in0[:, :, kc + c * span : kc + (c + 1) * span], c) for c in range(4)]
    out2 = jnp.concatenate([jnp.broadcast_to(coarse, (PLANE, ROWS, kc))] + pieces, axis=2)
    in2 = swap(out2, plane).reshape(PLANE * ROWS, -1)[:rows]
    coarse_res = in2[:, :kc]
    received = in2[:, kc:]
    lift = jnp.dot(coarse_inv, modes.T, precision=HI)
    pushed = jnp.einsum("ij,jx->ix", ghost_face, received.reshape(ndof, -1), precision=HI).reshape(rows, -1)
    pushed = pushed * weights[None, :]
    hit = (ids[:, None] == order[None, :]).astype(jnp.float32)
    margin = (layers[:, None] == order[None, :]).astype(jnp.float32)
    ordered = jnp.dot(both, hit, precision=HI) + jnp.dot(pushed, margin, precision=HI)
    results = []
    spot = ids % LINE
    first_of = spot[None, :] > 0
    last_of = spot[None, :] < LINE - 1
    split = ordered.reshape(ndof, apps, count)
    for app in range(apps):
        mine = split[:, app]
        first = jnp.einsum("ijp,jp->ip", block_inv, mine, precision=HI)
        before = jnp.where(first_of, jnp.roll(first, 1, axis=1), 0.0)
        after = jnp.where(last_of, jnp.roll(first, -1, axis=1), 0.0)
        coupled = mine + line_coef[0] * jnp.dot(line_faces[0], before, precision=HI)
        coupled = coupled + line_coef[1] * jnp.dot(line_faces[1], after, precision=HI)
        results.append(jnp.einsum("ijp,jp->ip", block_inv, coupled, precision=HI))
    second = jnp.stack(results, axis=1).reshape(rows, count)
    total = jnp.dot(second, hit.T, precision=HI) + jnp.dot(coarse_res, lift, precision=HI)
    return jnp.transpose(total.reshape(ndof, apps, count), (1, 0, 2))


def solution(mesh):
    in_specs = (
        P(None, None, ALL),
        P(None, None, ALL),
        P(ALL, None),
        P(None, ALL),
        P(),
        P(ALL, None, None),
        P(ALL, None, None),
        P(),
        P(ALL, None),
        P(),
    )
    out_specs = P(None, None, ALL)
    return jax.shard_map(shards, mesh=mesh, in_specs=in_specs, out_specs=out_specs, check_vma=False)
```

```python
import jax
import jax.numpy as jnp
import numpy as np
from jax import lax
from jax.experimental import pallas as pl
from jax.experimental.pallas import tpu as pltpu
from jax.sharding import PartitionSpec as P

LINE = 32
ALL = ("wide", "narrow")
PLANE = 32
RING = 16
ROWS = 4
PAD = 56
BLOCKS = 2 * PAD // ROWS
HI = lax.Precision.HIGHEST
F32 = jnp.float32
BF16 = jnp.bfloat16
VMEM = pl.BlockSpec(memory_space=pltpu.VMEM)


def groups():
    place = np.arange(PLANE * RING).reshape(2, PLANE, 8)
    plane = place.transpose(0, 2, 1).reshape(-1, PLANE).tolist()
    ring = place.transpose(1, 0, 2).reshape(-1, RING).tolist()
    return plane, ring


def swap(blocks, groups_of):
    return lax.all_to_all(blocks, ALL, 0, 0, axis_index_groups=groups_of)


def flip(blocks, colour):
    half = 1 << colour
    shape = blocks.shape
    return blocks.reshape((-1, 2, half) + shape[1:])[:, ::-1].reshape(shape)


def halves(x):
    high = x.astype(BF16)
    return high, (x - high.astype(F32)).astype(BF16)


def mul(a, b):
    return jnp.dot(a, b, preferred_element_type=F32)


def product(a, b):
    ah, al = halves(a)
    bh, bl = halves(b)
    n = a.shape[0]
    both = mul(jnp.concatenate([ah, al], axis=0), bh)
    return both[:n] + both[n:] + mul(ah, bl)


def choose(a, hit):
    ah, al = halves(a)
    n = a.shape[0]
    both = mul(jnp.concatenate([ah, al], axis=0), hit)
    return both[:n] + both[n:]


def one_hot(flags):
    return jnp.where(flags, 1.0, 0.0).astype(BF16)


def load_rows(x_ref, stack):
    ndof = x_ref.shape[0]
    stack[...] = jnp.zeros_like(stack)
    for app in range(2):
        stack[PAD * app : PAD * app + ndof, :] = x_ref[:, app, :]
    return stack[...]


def front_kernel(x_ref, modes_ref, layers_ref, out_ref, stack, wide):
    x = load_rows(x_ref, stack)
    count = x.shape[1]
    kc = modes_ref.shape[1]
    span = layers_ref.shape[1]
    wide[:, :kc] = product(x, modes_ref[...])
    ids = lax.broadcasted_iota(jnp.int32, (count, span), 0)
    for c in range(4):
        wide[:, kc + c * span : kc + (c + 1) * span] = choose(x, one_hot(ids == layers_ref[c : c + 1, :]))
    for k in range(BLOCKS):
        out_ref[k] = wide[ROWS * k : ROWS * k + ROWS, :]
    for k in range(BLOCKS, PLANE):
        out_ref[k] = jnp.zeros(out_ref.shape[1:], F32)


def front(x3, modes, layers):
    width = modes.shape[1] + layers.size
    return pl.pallas_call(
        front_kernel,
        out_shape=jax.ShapeDtypeStruct((PLANE, ROWS, width), F32),
        in_specs=[VMEM] * 3,
        scratch_shapes=[pltpu.VMEM((2 * PAD, x3.shape[2]), F32), pltpu.VMEM((2 * PAD, width), F32)],
        name="front",
    )(x3, modes, layers)


def solve(blocks_ref, x):
    ndof, _, count = blocks_ref.shape
    rows = []
    for i in range(ndof):
        block = blocks_ref[i]
        left = jnp.sum(block * x[:, :count], axis=0, keepdims=True)
        right = jnp.sum(block * x[:, count:], axis=0, keepdims=True)
        rows.append(jnp.concatenate([left, right], axis=1))
    return jnp.concatenate(rows, axis=0)


def tail_kernel(
    in_ref, x_ref, blocks_ref, order_ref, coef_ref, faces_ref, layers_ref, weights_ref, ghost_ref, lift_ref,
    out_ref, stack, wide,
):
    ndof, _, count = x_ref.shape
    kc = lift_ref.shape[0]
    x = load_rows(x_ref, stack)
    for k in range(BLOCKS):
        wide[ROWS * k : ROWS * k + ROWS, :] = in_ref[k]
    span = layers_ref.shape[0]
    received = jnp.concatenate([wide[PAD * a : PAD * a + ndof, kc:] for a in range(2)], axis=1)
    pushed = product(ghost_ref[...], received)
    weights = weights_ref[...]
    zero = jnp.zeros((PAD - ndof, span), F32)
    pushed = jnp.concatenate(
        [pushed[:, :span] * weights, zero, pushed[:, span:] * weights, zero], axis=0
    )
    order = order_ref[...]
    hit = one_hot(lax.broadcasted_iota(jnp.int32, (count, count), 0) == order)
    margin = one_hot(layers_ref[...] == order)
    ordered = choose(x, hit) + choose(pushed, margin)
    ordered = jnp.concatenate([ordered[:ndof], ordered[PAD : PAD + ndof]], axis=1)
    first = solve(blocks_ref, ordered)
    spot = lax.broadcasted_iota(jnp.int32, (1, count), 1) % LINE
    before = jnp.where(spot > 0, coef_ref[0:1, :], 0.0)
    after = jnp.where(spot < LINE - 1, coef_ref[1:2, :], 0.0)
    ahead = product(faces_ref[0], first)
    behind = product(faces_ref[1], first)
    coupled = []
    for a in range(2):
        cut = slice(a * count, a * count + count)
        coupled.append(
            ordered[:, cut]
            + before * pltpu.roll(ahead[:, cut], 1, 1)
            + after * pltpu.roll(behind[:, cut], count - 1, 1)
        )
    second = solve(blocks_ref, jnp.concatenate(coupled, axis=1))
    hole = jnp.zeros((PAD - ndof, count), F32)
    second = jnp.concatenate([second[:, :count], hole, second[:, count:], hole], axis=0)
    back = one_hot(lax.broadcasted_iota(jnp.int32, (count, count), 0) == order)
    sh, sl = halves(second)
    turned = lax.dot_general(
        jnp.concatenate([sh, sl], axis=0), back, (((1,), (1,)), ((), ())), preferred_element_type=F32
    )
    total = turned[: 2 * PAD] + turned[2 * PAD :] + product(wide[:, :kc], lift_ref[...])
    for a in range(2):
        out_ref[:, a, :] = total[PAD * a : PAD * a + ndof]


def tail(in2, x3, blocks, order, coef, faces, layers, weights, ghost, lift):
    ndof, apps, count = x3.shape
    return pl.pallas_call(
        tail_kernel,
        out_shape=jax.ShapeDtypeStruct(x3.shape, F32),
        in_specs=[VMEM] * 10,
        scratch_shapes=[pltpu.VMEM((2 * PAD, count), F32), pltpu.VMEM((2 * PAD, in2.shape[2]), F32)],
        name="tail",
    )(in2, x3, blocks, order, coef, faces, layers, weights, ghost, lift)


def shards(
    rhs,
    block_inv,
    line_order,
    line_coef,
    line_faces,
    intersection,
    intersection_coef,
    ghost_face,
    modes,
    coarse_inv,
):
    plane, ring = groups()
    kc = modes.shape[1]
    span = intersection.shape[2]
    x3 = jnp.transpose(rhs, (1, 0, 2))
    in0 = swap(front(x3, modes, intersection[0]), plane)
    part = jnp.sum(in0[:, :, :kc], axis=0)
    in1 = swap(jnp.broadcast_to(part, (RING, ROWS, kc)), ring)
    pieces = [flip(in0[:, :, kc + c * span : kc + (c + 1) * span], c) for c in range(4)]
    base = jnp.concatenate([jnp.zeros((PLANE, ROWS, kc), F32)] + pieces, axis=2)
    coarse = jnp.sum(in1, axis=0)
    out2 = lax.dynamic_update_slice(base, jnp.broadcast_to(coarse, (PLANE, ROWS, kc)), (0, 0, 0))
    in2 = swap(out2, plane)
    lift = jnp.dot(coarse_inv, modes.T, precision=HI)
    out = tail(
        in2,
        x3,
        block_inv,
        line_order,
        line_coef,
        line_faces,
        intersection.reshape(-1, 1),
        intersection_coef.reshape(1, -1),
        ghost_face,
        lift,
    )
    return jnp.transpose(out, (1, 0, 2))


def solution(mesh):
    in_specs = (
        P(None, None, ALL),
        P(None, None, ALL),
        P(ALL, None),
        P(None, ALL),
        P(),
        P(ALL, None, None),
        P(ALL, None, None),
        P(),
        P(ALL, None),
        P(),
    )
    out_specs = P(None, None, ALL)
    return jax.shard_map(shards, mesh=mesh, in_specs=in_specs, out_specs=out_specs, check_vma=False)
```

```python
import jax
import jax.numpy as jnp
import numpy as np
from jax import lax
from jax.experimental import pallas as pl
from jax.experimental.pallas import tpu as pltpu
from jax.sharding import PartitionSpec as P


LINE = 32
ALL = ("wide", "narrow")
PLANE = 32
RING = 16
ROWS = 4
PAD = 56
BLOCKS = 2 * PAD // ROWS
F32 = jnp.float32
BF16 = jnp.bfloat16
GRANT = 16 << 20


def groups():
    place = np.arange(PLANE * RING).reshape(2, PLANE, 8)
    plane = place.transpose(0, 2, 1).reshape(-1, PLANE).tolist()
    ring = place.transpose(1, 0, 2).reshape(-1, RING).tolist()
    return plane, ring


def swap(blocks, groups_of):
    return lax.all_to_all(blocks, ALL, 0, 0, axis_index_groups=groups_of)


def partner(block, colour):
    count = lax.axis_size("wide")
    return lax.ppermute(block, "wide", [(i, i ^ 1 << colour) for i in range(count)])


def halves(x):
    high = x.astype(BF16)
    return high, (x - high.astype(F32)).astype(BF16)


def mul(a, b):
    return jnp.dot(a, b, preferred_element_type=F32)


def product(a, b):
    ah, al = halves(a)
    bh, bl = halves(b)
    n = a.shape[0]
    both = mul(jnp.concatenate([ah, al], axis=0), bh)
    return both[:n] + both[n:] + mul(ah, bl)


def choose(a, hit):
    ah, al = halves(a)
    n = a.shape[0]
    both = mul(jnp.concatenate([ah, al], axis=0), hit)
    return both[:n] + both[n:]


def one_hot(flags):
    return jnp.where(flags, 1.0, 0.0).astype(BF16)


def near(x):
    return pltpu.with_memory_space_constraint(x, pltpu.VMEM)


def far(*arrays):
    return [pltpu.with_memory_space_constraint(x, pltpu.HBM) for x in arrays]


def picks(layers_ref, count):
    ids = lax.broadcasted_iota(jnp.int32, (count, layers_ref.shape[1]), 0)
    return [one_hot(ids == layers_ref[c : c + 1, :]) for c in range(layers_ref.shape[0])]


def choose_back(a, hit):
    n = a.shape[0]
    both = jnp.concatenate(halves(a), axis=0)
    both = lax.dot_general(both, hit, (((1,), (1,)), ((), ())), preferred_element_type=F32)
    return both[:n] + both[n:]


def load_rows(x_ref, stack):
    ndof = x_ref.shape[0]
    stack[...] = jnp.zeros_like(stack)
    for app in range(2):
        stack[PAD * app : PAD * app + ndof, :] = x_ref[:, app, :]
    return stack[...]


def coarse_kernel(x_ref, modes_ref, out_ref, stack, wide):
    wide[...] = product(load_rows(x_ref, stack), modes_ref[...])
    for k in range(BLOCKS):
        out_ref[k] = wide[ROWS * k : ROWS * k + ROWS, :]
    for k in range(BLOCKS, PLANE):
        out_ref[k] = jnp.zeros(out_ref.shape[1:], F32)


def coarse_part(x3, modes):
    kc = modes.shape[1]
    return pl.pallas_call(
        coarse_kernel,
        out_shape=jax.ShapeDtypeStruct((PLANE, ROWS, kc), F32),
        scratch_shapes=[pltpu.VMEM((2 * PAD, x3.shape[2]), F32), pltpu.VMEM((2 * PAD, kc), F32)],
        compiler_params=pltpu.CompilerParams(vmem_limit_bytes=GRANT),
        name="coarse",
    )(*far(x3, modes))


def layer_kernel(x_ref, layers_ref, *rest):
    *outs, stack = rest
    x = load_rows(x_ref, stack)
    for out_ref, hit in zip(outs, picks(layers_ref, x.shape[1])):
        out_ref[...] = choose(x, hit)


def layer_parts(x3, layers):
    colours, span = layers.shape
    return pl.pallas_call(
        layer_kernel,
        out_shape=[jax.ShapeDtypeStruct((2 * PAD, span), F32)] * colours,
        scratch_shapes=[pltpu.VMEM((2 * PAD, x3.shape[2]), F32)],
        compiler_params=pltpu.CompilerParams(vmem_limit_bytes=GRANT),
        name="layers",
    )(*far(x3, layers))


def solve(blocks_ref, x):
    ndof, _, count = blocks_ref.shape
    rows = []
    for i in range(ndof):
        block = blocks_ref[i]
        left = jnp.sum(block * x[:, :count], axis=0, keepdims=True)
        right = jnp.sum(block * x[:, count:], axis=0, keepdims=True)
        rows.append(jnp.concatenate([left, right], axis=1))
    return jnp.concatenate(rows, axis=0)


def local_kernel(
    r0_ref, r1_ref, r2_ref, r3_ref, x_ref, blocks_hbm, order_ref, coef_ref, faces_ref, layers_ref, weights_ref,
    ghost_ref, out_ref, stack, blocks_ref, arrival,
):
    fetch = pltpu.make_async_copy(blocks_hbm, blocks_ref, arrival)
    fetch.start()
    ndof, _, count = x_ref.shape
    x = load_rows(x_ref, stack)
    span = layers_ref.size
    received = jnp.concatenate(
        [r_ref[PAD * a : PAD * a + ndof, :] for a in range(2) for r_ref in (r0_ref, r1_ref, r2_ref, r3_ref)], axis=1
    )
    pushed = product(ghost_ref[...], received)
    weights = weights_ref[...]
    zero = jnp.zeros((PAD - ndof, span), F32)
    pushed = jnp.concatenate(
        [pushed[:, :span] * weights, zero, pushed[:, span:] * weights, zero], axis=0
    )
    order = order_ref[...]
    hit = one_hot(lax.broadcasted_iota(jnp.int32, (count, count), 0) == order)
    boosted = x + choose_back(pushed, jnp.concatenate(picks(layers_ref, count), axis=1))
    ordered = choose(boosted, hit)
    ordered = jnp.concatenate([ordered[:ndof], ordered[PAD : PAD + ndof]], axis=1)
    fetch.wait()
    first = solve(blocks_ref, ordered)
    spot = lax.broadcasted_iota(jnp.int32, (1, count), 1) % LINE
    before = jnp.where(spot > 0, coef_ref[0:1, :], 0.0)
    after = jnp.where(spot < LINE - 1, coef_ref[1:2, :], 0.0)
    ahead = product(faces_ref[:, 0, :], first)
    behind = product(faces_ref[:, 1, :], first)
    coupled = []
    for a in range(2):
        cut = slice(a * count, a * count + count)
        coupled.append(
            ordered[:, cut]
            + before * pltpu.roll(ahead[:, cut], 1, 1)
            + after * pltpu.roll(behind[:, cut], count - 1, 1)
        )
    second = solve(blocks_ref, jnp.concatenate(coupled, axis=1))
    hole = jnp.zeros((PAD - ndof, count), F32)
    second = jnp.concatenate([second[:, :count], hole, second[:, count:], hole], axis=0)
    out_ref[...] = choose_back(second, hit)


def local_part(received, x3, blocks, order, coef, faces, layers, weights, ghost):
    count = x3.shape[2]
    near_spec = pl.BlockSpec(memory_space=pltpu.VMEM)
    return pl.pallas_call(
        local_kernel,
        out_shape=jax.ShapeDtypeStruct((2 * PAD, count), F32),
        in_specs=[near_spec] * 5 + [pl.BlockSpec(memory_space=pltpu.HBM)] + [near_spec] * 6,
        scratch_shapes=[
            pltpu.VMEM((2 * PAD, count), F32),
            pltpu.VMEM(blocks.shape, F32),
            pltpu.SemaphoreType.DMA(()),
        ],
        compiler_params=pltpu.CompilerParams(vmem_limit_bytes=GRANT),
        name="local",
    )(*map(near, received), *far(x3, blocks, order, coef, faces, layers, weights, ghost))


def lift_kernel(inv_ref, modes_ref, high_ref, low_ref):
    ah, al = halves(inv_ref[...])
    bh, bl = halves(modes_ref[...])
    turn = (((1,), (1,)), ((), ()))
    by = lambda u, v: lax.dot_general(u, v, turn, preferred_element_type=F32)
    high_ref[...], low_ref[...] = halves(by(ah, bh) + by(al, bh) + by(ah, bl))


def lift_part(coarse_inv, modes):
    shape = jax.ShapeDtypeStruct((modes.shape[1], modes.shape[0]), BF16)
    return pl.pallas_call(
        lift_kernel,
        out_shape=(shape, shape),
        compiler_params=pltpu.CompilerParams(vmem_limit_bytes=GRANT),
        name="lift",
    )(*far(coarse_inv, modes))


def last_kernel(coarse_ref, local_ref, high_ref, low_ref, out_ref, stack):
    ndof = out_ref.shape[0]
    for k in range(BLOCKS):
        stack[ROWS * k : ROWS * k + ROWS, :] = coarse_ref[k]
    ah, al = halves(stack[...])
    both = mul(jnp.concatenate([ah, al], axis=0), high_ref[...])
    total = local_ref[...] + both[: 2 * PAD] + both[2 * PAD :] + mul(ah, low_ref[...])
    for a in range(2):
        out_ref[:, a, :] = total[PAD * a : PAD * a + ndof]


def last(coarse, local, high, low, ndof):
    return pl.pallas_call(
        last_kernel,
        out_shape=jax.ShapeDtypeStruct((ndof, 2, local.shape[1]), F32),
        scratch_shapes=[pltpu.VMEM((2 * PAD, coarse.shape[2]), F32)],
        compiler_params=pltpu.CompilerParams(vmem_limit_bytes=GRANT),
        name="last",
    )(near(coarse), near(local), near(high), near(low))


def shards(
    rhs,
    block_inv,
    line_order,
    line_coef,
    line_faces,
    intersection,
    intersection_coef,
    ghost_face,
    modes,
    coarse_inv,
):
    plane, ring = groups()
    kc = modes.shape[1]
    x3 = jnp.transpose(rhs, (1, 0, 2))
    in0 = swap(coarse_part(x3, modes), plane)
    sent = layer_parts(x3, intersection[0])
    received = []
    for colour, block in enumerate(sent):
        received.append(partner(block, colour))
    part = jnp.sum(in0, axis=0)
    in1 = swap(jnp.broadcast_to(part, (RING, ROWS, kc)), ring)
    coarse = jnp.sum(in1, axis=0)
    in2 = swap(jnp.broadcast_to(coarse, (PLANE, ROWS, kc)), plane)
    high, low = lift_part(coarse_inv, modes)
    local = local_part(
        received,
        x3,
        block_inv,
        line_order,
        line_coef,
        jnp.transpose(line_faces, (1, 0, 2)),
        intersection[0],
        intersection_coef.reshape(1, -1),
        ghost_face,
    )
    out = last(in2, local, high, low, rhs.shape[1])
    return jnp.transpose(out, (1, 0, 2))


def solution(mesh):
    in_specs = (
        P(None, None, ALL),
        P(None, None, ALL),
        P(ALL, None),
        P(None, ALL),
        P(),
        P(ALL, None, None),
        P(ALL, None, None),
        P(),
        P(ALL, None),
        P(),
    )
    out_specs = P(None, None, ALL)
    return jax.shard_map(shards, mesh=mesh, in_specs=in_specs, out_specs=out_specs, check_vma=False)
```

```python
import jax
import jax.numpy as jnp
import numpy as np
from jax import lax
from jax.experimental import pallas as pl
from jax.experimental.pallas import tpu as pltpu
from jax.sharding import PartitionSpec as P


LINE = 32
ALL = ("wide", "narrow")
PLANE = 32
RING = 16
PAD = 56
LANES = 128
F32 = jnp.float32
BF16 = jnp.bfloat16
GRANT = 16 << 20


def groups():
    place = np.arange(PLANE * RING).reshape(2, PLANE, 8)
    plane = place.transpose(0, 2, 1).reshape(-1, PLANE)
    plane = plane[:, np.arange(PLANE).reshape(4, 4, 2).transpose(1, 0, 2).reshape(-1)[::-1]].tolist()
    ring = place.transpose(1, 0, 2).reshape(-1, RING)
    ring = ring[:, np.arange(RING) * 7 % RING].tolist()
    return plane, ring


def swap(blocks, groups_of):
    return lax.all_to_all(blocks, ALL, 0, 0, axis_index_groups=groups_of)


def partner(block, colour):
    count = lax.axis_size("wide")
    return lax.ppermute(block, "wide", [(i, i ^ 1 << colour) for i in range(count)])


def halves(x):
    high = x.astype(BF16)
    return high, (x - high.astype(F32)).astype(BF16)


def mul(a, b):
    return jnp.dot(a, b, preferred_element_type=F32)


def product(a, b):
    ah, al = halves(a)
    bh, bl = halves(b)
    n = a.shape[0]
    both = mul(jnp.concatenate([ah, al], axis=0), bh)
    return both[:n] + both[n:] + mul(ah, bl)


def choose(a, hit):
    ah, al = halves(a)
    n = a.shape[0]
    both = mul(jnp.concatenate([ah, al], axis=0), hit)
    return both[:n] + both[n:]


def one_hot(flags):
    return jnp.where(flags, 1.0, 0.0).astype(BF16)


def near(x):
    return pltpu.with_memory_space_constraint(x, pltpu.VMEM)


def far(*arrays):
    return [pltpu.with_memory_space_constraint(x, pltpu.HBM) for x in arrays]


def picks(layers_ref, count):
    ids = lax.broadcasted_iota(jnp.int32, (count, layers_ref.shape[1]), 0)
    return [one_hot(ids == layers_ref[c : c + 1, :]) for c in range(layers_ref.shape[0])]


def choose_back(a, hit):
    n = a.shape[0]
    both = jnp.concatenate(halves(a), axis=0)
    both = lax.dot_general(both, hit, (((1,), (1,)), ((), ())), preferred_element_type=F32)
    return both[:n] + both[n:]


def deal(rows, width):
    tiles = width // LANES
    full = rows // PLANE
    rest = rows - full * PLANE
    moves = [
        (slice(0, PLANE), b * tiles + c, slice(b * PLANE, b * PLANE + PLANE), c) for b in range(full) for c in range(tiles)
    ]
    moves += [(slice(rest * c, rest * c + rest), full * tiles, slice(full * PLANE, rows), c) for c in range(tiles)]
    return [
        (place, slice(LANES * slot, LANES * slot + LANES), of, slice(LANES * c, LANES * c + LANES))
        for place, slot, of, c in moves
    ]


def dealt(rows, width):
    tiles = width // LANES
    assert rows % PLANE * tiles <= PLANE
    return (rows // PLANE * tiles + 1) * LANES


def load_rows(x_ref, stack):
    ndof = x_ref.shape[0]
    stack[...] = jnp.zeros_like(stack)
    for app in range(2):
        stack[PAD * app : PAD * app + ndof, :] = x_ref[:, app, :]
    return stack[...]


def front_kernel(x_ref, modes_ref, layers_ref, out_ref, *rest):
    *sent, stack, wide = rest
    x = load_rows(x_ref, stack)
    ndof = x_ref.shape[0]
    coarse = product(x, modes_ref[...])
    wide[:ndof, :] = coarse[:ndof]
    wide[ndof : 2 * ndof, :] = coarse[PAD : PAD + ndof]
    out_ref[:, 0, out_ref.shape[2] - LANES :] = jnp.zeros((PLANE, LANES), F32)
    for place, slot, of, lanes in deal(2 * ndof, coarse.shape[1]):
        out_ref[place, 0, slot] = wide[of, lanes]
    for sent_ref, hit in zip(sent, picks(layers_ref, x.shape[1])):
        sent_ref[...] = choose(x, hit)


def front(x3, modes, layers):
    kc = modes.shape[1]
    colours, span = layers.shape
    return pl.pallas_call(
        front_kernel,
        out_shape=[jax.ShapeDtypeStruct((PLANE, 1, dealt(2 * x3.shape[0], kc)), F32)]
        + [jax.ShapeDtypeStruct((2 * PAD, span), F32)] * colours,
        scratch_shapes=[pltpu.VMEM((2 * PAD, x3.shape[2]), F32), pltpu.VMEM((2 * PAD, kc), F32)],
        compiler_params=pltpu.CompilerParams(vmem_limit_bytes=GRANT),
        name="front",
    )(*far(x3, modes, layers))


def solve(blocks_ref, x):
    ndof, _, count = blocks_ref.shape
    rows = []
    for i in range(ndof):
        block = blocks_ref[i]
        left = jnp.sum(block * x[:, :count], axis=0, keepdims=True)
        right = jnp.sum(block * x[:, count:], axis=0, keepdims=True)
        rows.append(jnp.concatenate([left, right], axis=1))
    return jnp.concatenate(rows, axis=0)


def local_kernel(
    r0_ref, r1_ref, r2_ref, r3_ref, x_ref, blocks_hbm, inv_hbm, modes_hbm, order_ref, coef_ref, faces_ref, layers_ref,
    weights_ref, ghost_ref, out_ref, high_ref, low_ref, stack, blocks_ref, inv_ref, modes_ref, arrival, arrival2, arrival3,
):
    fetch = pltpu.make_async_copy(blocks_hbm, blocks_ref, arrival)
    fetch.start()
    fetch2 = pltpu.make_async_copy(inv_hbm, inv_ref, arrival2)
    fetch2.start()
    fetch3 = pltpu.make_async_copy(modes_hbm, modes_ref, arrival3)
    fetch3.start()
    ndof, _, count = x_ref.shape
    x = load_rows(x_ref, stack)
    span = layers_ref.size
    received = jnp.concatenate(
        [r_ref[PAD * a : PAD * a + ndof, :] for a in range(2) for r_ref in (r0_ref, r1_ref, r2_ref, r3_ref)], axis=1
    )
    pushed = product(ghost_ref[...], received)
    weights = weights_ref[...]
    zero = jnp.zeros((PAD - ndof, span), F32)
    pushed = jnp.concatenate(
        [pushed[:, :span] * weights, zero, pushed[:, span:] * weights, zero], axis=0
    )
    order = order_ref[...]
    hit = one_hot(lax.broadcasted_iota(jnp.int32, (count, count), 0) == order)
    boosted = x + choose_back(pushed, jnp.concatenate(picks(layers_ref, count), axis=1))
    ordered = choose(boosted, hit)
    ordered = jnp.concatenate([ordered[:ndof], ordered[PAD : PAD + ndof]], axis=1)
    fetch.wait()
    first = solve(blocks_ref, ordered)
    spot = lax.broadcasted_iota(jnp.int32, (1, count), 1) % LINE
    before = jnp.where(spot > 0, coef_ref[0:1, :], 0.0)
    after = jnp.where(spot < LINE - 1, coef_ref[1:2, :], 0.0)
    ahead = product(faces_ref[:, 0, :], first)
    behind = product(faces_ref[:, 1, :], first)
    coupled = []
    for a in range(2):
        cut = slice(a * count, a * count + count)
        coupled.append(
            ordered[:, cut]
            + before * pltpu.roll(ahead[:, cut], 1, 1)
            + after * pltpu.roll(behind[:, cut], count - 1, 1)
        )
    second = solve(blocks_ref, jnp.concatenate(coupled, axis=1))
    hole = jnp.zeros((PAD - ndof, count), F32)
    second = jnp.concatenate([second[:, :count], hole, second[:, count:], hole], axis=0)
    out_ref[...] = choose_back(second, hit)
    fetch2.wait()
    fetch3.wait()
    ah, al = halves(inv_ref[...])
    bh, bl = halves(modes_ref[...])
    turn = (((1,), (1,)), ((), ()))
    by = lambda u, v: lax.dot_general(u, v, turn, preferred_element_type=F32)
    high_ref[...], low_ref[...] = halves(by(ah, bh) + by(al, bh) + by(ah, bl))


def local_part(received, x3, blocks, coarse_inv, modes, order, coef, faces, layers, weights, ghost):
    count, kc = modes.shape
    near_spec = pl.BlockSpec(memory_space=pltpu.VMEM)
    far_spec = pl.BlockSpec(memory_space=pltpu.HBM)
    lift = jax.ShapeDtypeStruct((kc, count), BF16)
    return pl.pallas_call(
        local_kernel,
        out_shape=[jax.ShapeDtypeStruct((2 * PAD, count), F32), lift, lift],
        in_specs=[near_spec] * 5 + [far_spec] * 3 + [near_spec] * 6,
        scratch_shapes=[
            pltpu.VMEM((2 * PAD, count), F32),
            pltpu.VMEM(blocks.shape, F32),
            pltpu.VMEM(coarse_inv.shape, F32),
            pltpu.VMEM(modes.shape, F32),
            pltpu.SemaphoreType.DMA(()),
            pltpu.SemaphoreType.DMA(()),
            pltpu.SemaphoreType.DMA(()),
        ],
        compiler_params=pltpu.CompilerParams(vmem_limit_bytes=GRANT),
        name="local",
    )(*map(near, received), *far(x3, blocks, coarse_inv, modes, order, coef, faces, layers, weights, ghost))


def spread_kernel(in_ref, out_ref):
    total = jnp.sum(in_ref[:, 0, :], axis=0, keepdims=True)
    out_ref[:, 0, :] = jnp.broadcast_to(total, (out_ref.shape[0], total.shape[1]))


def spread_sum(blocks, copies):
    return pl.pallas_call(
        spread_kernel,
        out_shape=jax.ShapeDtypeStruct((copies,) + blocks.shape[1:], F32),
        compiler_params=pltpu.CompilerParams(vmem_limit_bytes=GRANT),
        name="spread_sum",
    )(near(blocks))


def last_kernel(coarse_ref, local_ref, high_ref, low_ref, out_ref, stack):
    ndof = out_ref.shape[0]
    stack[2 * ndof :, :] = jnp.zeros((2 * PAD - 2 * ndof, stack.shape[1]), F32)
    for place, slot, of, lanes in deal(2 * ndof, stack.shape[1]):
        stack[of, lanes] = coarse_ref[place, 0, slot]
    ah, al = halves(stack[...])
    both = mul(jnp.concatenate([ah, al], axis=0), high_ref[...])
    total = both[: 2 * PAD] + both[2 * PAD :] + mul(ah, low_ref[...])
    for a in range(2):
        out_ref[:, a, :] = local_ref[PAD * a : PAD * a + ndof, :] + total[ndof * a : ndof * a + ndof]


def last(coarse, local, high, low, ndof):
    return pl.pallas_call(
        last_kernel,
        out_shape=jax.ShapeDtypeStruct((ndof, 2, local.shape[1]), F32),
        scratch_shapes=[pltpu.VMEM((2 * PAD, high.shape[0]), F32)],
        compiler_params=pltpu.CompilerParams(vmem_limit_bytes=GRANT),
        name="last",
    )(near(coarse), near(local), near(high), near(low))


def shards(
    rhs,
    block_inv,
    line_order,
    line_coef,
    line_faces,
    intersection,
    intersection_coef,
    ghost_face,
    modes,
    coarse_inv,
):
    plane, ring = groups()
    x3 = jnp.transpose(rhs, (1, 0, 2))
    first, *sent = front(x3, modes, intersection[0])
    in0 = swap(first, plane)
    received = []
    for colour, block in enumerate(sent):
        received.append(partner(block, colour))
    zin = spread_sum(in0, RING)
    in1 = swap(zin, ring)
    back = spread_sum(in1, PLANE)
    in2 = swap(back, plane)
    local, high, low = local_part(
        received,
        x3,
        block_inv,
        coarse_inv,
        modes,
        line_order,
        line_coef,
        jnp.transpose(line_faces, (1, 0, 2)),
        intersection[0],
        intersection_coef.reshape(1, -1),
        ghost_face,
    )
    out = last(in2, local, high, low, rhs.shape[1])
    return jnp.transpose(out, (1, 0, 2))


def solution(mesh):
    in_specs = (
        P(None, None, ALL),
        P(None, None, ALL),
        P(ALL, None),
        P(None, ALL),
        P(),
        P(ALL, None, None),
        P(ALL, None, None),
        P(),
        P(ALL, None),
        P(),
    )
    out_specs = P(None, None, ALL)
    return jax.shard_map(shards, mesh=mesh, in_specs=in_specs, out_specs=out_specs, check_vma=False)
```
